512 devices in a mesh: slab: 64 (over x, y, z_lo), col: 8 (over z_hi, core).
Axes of the slice: x: 4, y: 8, z: 8 (z_hi: 4, z_lo: 2; z = z_hi * 2 + z_lo), core: 2. Of those that a mesh axis runs over, the one named last changes fastest.
Arguments:
- green_blocks: float32 [64, 2, 2048, 2048], P('slab', None, None, 'col'), may hold values from -0.125 to 0.125
- traces: float32 [64, 2, 64, 2048], P('slab', None, None, 'col'), may hold values from -6 to 6
- sources: float32 [64, 2, 64, 2048], P('slab', None, None, 'col'), may hold values from -6 to 6
Outputs:
- swept: float32 [64, 2, 64, 2048], P('slab', None, None, 'col')
The draws below stay inside these ranges and needn't reach their ends.
All inputs are finite; a program needn't handle non-finite values.
Results may differ from the reference program's by a relative error of at most 0.00014.
Values sent between devices are 32-bit elements; how exact they have to be, the bound alone decides.
A program may use at most 64 MiB of HBM per device.

```python
import jax
import jax.numpy as jnp
from jax import lax

C = 2048
SHOTS = 64
STEPS = 4
SLABS = 64


def strengthened(array, rng, source, target, blocks, factor):
    def block_of(dim):
        return (jnp.arange(array.shape[dim]) // (array.shape[dim] // blocks)).reshape((-1,) + (1,) * (array.ndim - 1 - dim))

    near = jax.random.permutation(rng, blocks)[block_of(target)]
    second = (block_of(target) + blocks // 2) % blocks
    return jnp.where((block_of(source) == near) | (block_of(source) == second), factor * array, array)


def steps_of(key, extent, pieces, smallest, top_value):
    def one(position, shards_of):
        heights = jax.random.uniform(jax.random.fold_in(jax.random.fold_in(key, 6), position), (shards_of,), jnp.float32, smallest / len(pieces), top_value / len(pieces))
        return jnp.repeat(jnp.exp(heights), extent[position] // shards_of).reshape((-1,) + (1,) * (len(extent) - position - 1))

    level = one(*pieces[0])
    for cut in pieces[1:]:
        level = level * one(*cut)
    return level


def centred(rng, shape, deviation, limit, pieces=(), held_as=jnp.bfloat16):
    drawn = jax.random.normal(rng, shape, jnp.float32) * deviation
    if len(pieces) > 0:
        drawn = steps_of(rng, shape, pieces, -0.22, 0.18) * drawn
    return jnp.clip(drawn, min=-limit, max=limit).astype(held_as)


def noise_with(rng, dims, width, reach, cuts, heavy, dtype=jnp.bfloat16):
    values = width * jax.random.normal(rng, dims, jnp.float32)
    if cuts:
        values = values * steps_of(rng, dims, cuts, -0.22, 0.18)
    return jnp.clip(strengthened(values, jax.random.fold_in(rng, 3), *heavy), -reach, reach).astype(dtype)


def setup_inputs(seed: int = 0) -> dict:
    arg_keys = jax.random.split(jax.random.key(seed), 4)
    green_blocks = noise_with(arg_keys[0], (SLABS, 2, C, C), (2 * C) ** -0.5, 0.125, ((0, 64), (3, 8)), (3, 2, 8, 2.0), jnp.float32)
    traces = centred(arg_keys[1], (SLABS, 2, SHOTS, C), 1.0, 6.0, ((0, 64), (3, 8)), jnp.float32)
    sources = centred(arg_keys[2], (SLABS, 2, SHOTS, C), 1.0, 6.0, ((0, 64), (3, 8)), jnp.float32)
    return dict(green_blocks=green_blocks, traces=traces, sources=sources)


def matmul_t(left, right):
    return lax.dot_general(left, right, (((1,), (1,)), ((), ())), precision=lax.Precision.HIGHEST, preferred_element_type=jnp.float32)


def one_slab(packed):
    matrix, incoming, own_source = packed
    real_out = matmul_t(incoming[0], matrix[0]) - matmul_t(incoming[1], matrix[1]) + own_source[0]
    imag_out = matmul_t(incoming[1], matrix[0]) + matmul_t(incoming[0], matrix[1]) + own_source[1]
    return jnp.stack([real_out, imag_out], 0)


def reference(green_blocks, traces, sources):
    current = traces
    for step_index in range(STEPS):
        from_above = jnp.concatenate([jnp.zeros_like(current[:1]), current[:-1]], 0)
        current = lax.map(one_slab, (green_blocks, from_above, sources))
    return current
```

```python
import jax
import jax.numpy as jnp
from jax import lax
from jax.experimental import pallas as pl
from jax.experimental.pallas import tpu as pltpu
from jax.sharding import PartitionSpec as P

STEPS = 4
GROUPS = 2
CHIPS = 4
MESH = pl.DeviceIdType.MESH
F32 = jnp.float32
BF16 = jnp.bfloat16

FAR_A, FAR_B, NEAR_A, NEAR_B = range(4)
LAST_FAR_A, LAST_FAR_B, LAST_DIRECT_A, LAST_DIRECT_B, LAST_SUM_A, LAST_SUM_B = range(6)


def pack(block, group):
    shots = pl.ds(32 * group, 32)
    rows = [block[part, shots, pl.ds(128 * half, 128)] for half in range(2) for part in range(2)]
    return jnp.concatenate(rows, 0).T


def split(value):
    high = value.astype(BF16)
    return high, (value - high.astype(F32)).astype(BF16)


def kernel(
    green, traces, sources, swept,
    staged, left, right, source_block, incoming, held, partner_held,
    far_out, far_in, near_own, near_out, near_in, last_own, last_out, last_in,
    green_local_sem, green_send_sem, green_recv_sem, source_sem, first_send_sem, first_recv_sem,
    share_send_sem, share_recv_sem, far_send_sem, far_recv_sem, near_send_sem, near_recv_sem,
    last_send_sem, last_recv_sem,
):
    slabs = lax.axis_size("slab")
    slab, col = lax.axis_index("slab"), lax.axis_index("col")
    chip, core = col // 2, col % 2
    sigma = 1 - 2 * (slab % 2)
    below, above = (slab + 1) % slabs, (slab + slabs - 1) % slabs
    ahead, behind, across = (chip + sigma + CHIPS) % CHIPS, (chip - sigma + CHIPS) % CHIPS, (chip + 2) % CHIPS
    at = lambda s, c, k=core: (s, 2 * c + k)
    partner = at(slab, chip, 1 - core)
    sent = []

    def send(source, target, send_sem, recv_sem, device):
        copy = pltpu.make_async_remote_copy(
            src_ref=source, dst_ref=target, send_sem=send_sem, recv_sem=recv_sem, device_id=device, device_id_type=MESH
        )
        copy.start()
        sent.append(copy)

    def arrived(target, recv_sem):
        pltpu.make_async_copy(target, target, recv_sem).wait()

    barrier = pltpu.get_barrier_semaphore()
    senders = (at(slab, ahead), at(slab, behind), partner, at(above, chip), at(above, behind))
    for device in senders:
        pl.semaphore_signal(barrier, inc=1, device_id=device, device_id_type=MESH)

    slot_chips = (ahead, across, chip, behind)

    def green_rows(slot, k):
        return green.at[0, :, pl.ds(pl.multiple_of(512 * slot_chips[slot] + 256 * k, 256), 256), :]

    local = []
    for slot in range(CHIPS):
        copy = pltpu.make_async_copy(green_rows(slot, core), staged.at[0, slot], green_local_sem.at[slot])
        copy.start()
        local.append(copy)
    source_copy = pltpu.make_async_copy(sources.at[0], source_block, source_sem)
    source_copy.start()

    pl.semaphore_wait(barrier, len(senders))
    for group in range(GROUPS):
        send(
            traces.at[0, :, pl.ds(32 * group, 32), :], incoming.at[group],
            first_send_sem.at[group], first_recv_sem.at[group], at(below, chip),
        )
    for slot in range(CHIPS):
        send(
            green_rows(slot, 1 - core), staged.at[1, slot], green_send_sem.at[slot], green_recv_sem.at[slot], partner
        )

    def convert(origin, slot):
        for part in range(2):
            for half in range(2):
                high, low = split(staged[origin, slot, part, pl.ds(128 * half, 128), :])
                columns = pl.ds(256 * ((part * 2 + origin) * 2 + half), 256)
                left[slot, pl.ds(0, 128), columns] = high
                left[slot, pl.ds(128, 128), columns] = low

    for slot in range(CHIPS):
        local[slot].wait()
        convert(0, slot)
    source_copy.wait()

    def share(step, group, value):
        value = jnp.where(slab == 0, jnp.zeros_like(value), value)
        held[step, group] = value
        send(
            held.at[step, group], partner_held.at[step, group],
            share_send_sem.at[step, group], share_recv_sem.at[step, group], partner,
        )

    lane = lax.broadcasted_iota(jnp.int32, (128, 128), 1)
    low_lanes = lane < 64
    real_lanes = lane % 64 < 32

    def make_right(step, group):
        arrived(partner_held.at[step, group], share_recv_sem.at[step, group])
        for origin in range(2):
            value = (held if origin == 0 else partner_held)[step, group]
            turned = jnp.where(real_lanes, -pltpu.roll(value, 96, 1), pltpu.roll(value, 32, 1))
            for part, term in ((0, value), (1, turned)):
                swapped = pltpu.roll(term, 64, 1)
                quarters = (
                    jnp.where(low_lanes, term, 0.0), jnp.where(low_lanes, swapped, 0.0),
                    jnp.where(low_lanes, 0.0, swapped), jnp.where(low_lanes, 0.0, term),
                )
                for index, quarter in enumerate(quarters):
                    high, low = split(quarter)
                    rows = pl.ds(256 * ((part * 2 + origin) * 2) + 128 * index, 128)
                    right[group, rows, pl.ds(0, 128)] = high
                    right[group, rows, pl.ds(128, 128)] = low

    def product(group, slot):
        full = jnp.dot(left[slot], right[group], preferred_element_type=F32)
        return (full[:128, :128] + full[:128, 128:]) + (full[128:, :128] + full[128:, 128:])

    def send_far(step, group):
        for slot, device in ((FAR_A, at(slab, ahead)), (FAR_B, at(slab, behind))):
            far_out[step, group, slot] = product(group, slot)
            send(
                far_out.at[step, group, slot], far_in.at[step, group, slot],
                far_send_sem.at[step, group, slot], far_recv_sem.at[step, group, slot], device,
            )

    def own_near(step, group):
        near_own[group, 0] = product(group, NEAR_A) + pack(source_block, group)
        near_own[group, 1] = product(group, NEAR_B)

    def send_near(step, group):
        for side, device in ((0, at(below, chip)), (1, at(below, behind))):
            arrived(far_in.at[step, group, side], far_recv_sem.at[step, group, side])
            near_out[step, group, side] = near_own[group, side] + far_in[step, group, side]
            send(
                near_out.at[step, group, side], near_in.at[step, group, side],
                near_send_sem.at[step, group, side], near_recv_sem.at[step, group, side], device,
            )

    def take_near(step, group):
        for side in range(2):
            arrived(near_in.at[step, group, side], near_recv_sem.at[step, group, side])
        share(step + 1, group, near_in[step, group, 0] + near_in[step, group, 1])

    def send_last(group, which, device):
        send(
            last_out.at[group, which], last_in.at[group, which],
            last_send_sem.at[group, which], last_recv_sem.at[group, which], device,
        )

    def last_products(group):
        forward, backward = at(slab, ahead), at(slab, behind)
        far = product(group, FAR_B)
        last_out[group, LAST_FAR_A] = far[:64]
        send_last(group, LAST_FAR_A, forward)
        last_out[group, LAST_FAR_B] = far[64:]
        send_last(group, LAST_FAR_B, backward)
        near = product(group, FAR_A)
        last_out[group, LAST_DIRECT_A] = near[64:]
        send_last(group, LAST_DIRECT_A, forward)
        last_own[group, pl.ds(0, 64)] = near[:64]
        near = product(group, NEAR_B)
        last_out[group, LAST_DIRECT_B] = near[:64]
        send_last(group, LAST_DIRECT_B, backward)
        last_own[group, pl.ds(64, 64)] = near[64:]
        near_own[group, 0] = product(group, NEAR_A) + pack(source_block, group)

    def last_relay(group):
        for side, device in ((0, at(slab, ahead)), (1, at(slab, behind))):
            far, out = LAST_FAR_A + side, LAST_SUM_A + side
            arrived(last_in.at[group, far], last_recv_sem.at[group, far])
            last_out[group, out] = last_own[group, pl.ds(64 * side, 64)] + last_in[group, far]
            send_last(group, out, device)

    def last_take(group):
        for which in (LAST_DIRECT_A, LAST_DIRECT_B, LAST_SUM_A, LAST_SUM_B):
            arrived(last_in.at[group, which], last_recv_sem.at[group, which])
        top = near_own[group, 0, pl.ds(0, 64)] + (last_in[group, LAST_SUM_A] + last_in[group, LAST_DIRECT_B])
        bottom = near_own[group, 0, pl.ds(64, 64)] + (last_in[group, LAST_SUM_B] + last_in[group, LAST_DIRECT_A])
        rows = jnp.concatenate([top, bottom], 0).T
        for half in range(2):
            for part in range(2):
                swept[0, part, pl.ds(32 * group, 32), pl.ds(128 * half, 128)] = rows[32 * (2 * half + part) :][:32]

    for group in range(GROUPS):
        arrived(incoming.at[group], first_recv_sem.at[group])
        share(0, group, pack(incoming.at[group], 0))
    for slot in range(CHIPS):
        arrived(staged.at[1, slot], green_recv_sem.at[slot])
        convert(1, slot)
    for group in range(GROUPS):
        make_right(0, group)
        send_far(0, group)
        own_near(0, group)
    for step in range(STEPS - 1):
        for group in range(GROUPS):
            send_near(step, group)
        for group in range(GROUPS):
            take_near(step, group)
            make_right(step + 1, group)
            if step + 1 < STEPS - 1:
                send_far(step + 1, group)
                own_near(step + 1, group)
            else:
                last_products(group)
    for group in range(GROUPS):
        last_relay(group)
    for group in range(GROUPS):
        last_take(group)
    for copy in sent:
        copy.wait_send()


def sweep(green_blocks, traces, sources):
    steps, dma = STEPS - 1, pltpu.SemaphoreType.DMA
    return pl.pallas_call(
        kernel,
        out_shape=jax.ShapeDtypeStruct(traces.shape, F32),
        in_specs=[pl.BlockSpec(memory_space=pl.ANY)] * 3,
        out_specs=pl.BlockSpec(memory_space=pltpu.VMEM),
        scratch_shapes=[
            pltpu.VMEM((2, CHIPS, 2, 256, 256), F32),
            pltpu.VMEM((CHIPS, 256, 2048), BF16),
            pltpu.VMEM((GROUPS, 2048, 256), BF16),
            pltpu.VMEM((2, 64, 256), F32),
            pltpu.VMEM((GROUPS, 2, 32, 256), F32),
            pltpu.VMEM((STEPS, GROUPS, 128, 128), F32),
            pltpu.VMEM((STEPS, GROUPS, 128, 128), F32),
            pltpu.VMEM((steps, GROUPS, 2, 128, 128), F32),
            pltpu.VMEM((steps, GROUPS, 2, 128, 128), F32),
            pltpu.VMEM((GROUPS, 2, 128, 128), F32),
            pltpu.VMEM((steps, GROUPS, 2, 128, 128), F32),
            pltpu.VMEM((steps, GROUPS, 2, 128, 128), F32),
            pltpu.VMEM((GROUPS, 128, 128), F32),
            pltpu.VMEM((GROUPS, 6, 64, 128), F32),
            pltpu.VMEM((GROUPS, 6, 64, 128), F32),
            dma((CHIPS,)), dma((CHIPS,)), dma((CHIPS,)), dma, dma((GROUPS,)), dma((GROUPS,)),
            dma((STEPS, GROUPS)), dma((STEPS, GROUPS)),
            dma((steps, GROUPS, 2)), dma((steps, GROUPS, 2)), dma((steps, GROUPS, 2)), dma((steps, GROUPS, 2)),
            dma((GROUPS, 6)), dma((GROUPS, 6)),
        ],
        compiler_params=pltpu.CompilerParams(
            collective_id=0, has_side_effects=True, vmem_limit_bytes=48 * 1024 * 1024
        ),
        name="sweep",
    )(green_blocks, traces, sources)


def solution(mesh):
    placed = P("slab", None, None, "col")
    return jax.shard_map(sweep, mesh=mesh, in_specs=(placed,) * 3, out_specs=placed, check_vma=False)
```

```python
import jax
import jax.numpy as jnp
from jax import lax
from jax.experimental import pallas as pl
from jax.experimental.pallas import tpu as pltpu
from jax.sharding import PartitionSpec as P

STEPS = 4
GROUPS = 2
CHIPS = 4
PIECES = 2
PIECE = 128 // PIECES
MESH = pl.DeviceIdType.MESH
F32 = jnp.float32
BF16 = jnp.bfloat16

FAR_A, FAR_B, NEAR_A, NEAR_B = range(4)
LAST_FAR_A, LAST_FAR_B, LAST_DIRECT_A, LAST_DIRECT_B, LAST_SUM_A, LAST_SUM_B = range(6)


def pack(block, group):
    shots = pl.ds(32 * group, 32)
    rows = [block[part, shots, pl.ds(128 * half, 128)] for half in range(2) for part in range(2)]
    return jnp.concatenate(rows, 0).T


def split(value):
    high = value.astype(BF16)
    return high, (value - high.astype(F32)).astype(BF16)


def kernel(
    green, traces, sources, swept,
    staged, left, right, source_block, incoming, held, partner_held,
    begun, far_out, far_in, near_own, near_out, near_in, last_own, last_out, last_in, last_near_out, last_near_in,
    green_local_sem, green_send_sem, green_recv_sem, source_send_sem, source_recv_sem, first_send_sem, first_recv_sem,
    share_send_sem, share_recv_sem, far_send_sem, far_recv_sem, near_send_sem, near_recv_sem,
    last_send_sem, last_recv_sem, last_near_send_sem, last_near_recv_sem,
):
    slabs = lax.axis_size("slab")
    slab, col = lax.axis_index("slab"), lax.axis_index("col")
    chip, core = col // 2, col % 2
    sigma = 1 - 2 * (slab % 2)
    below, above = (slab + 1) % slabs, (slab + slabs - 1) % slabs
    ahead, behind, across = (chip + sigma + CHIPS) % CHIPS, (chip - sigma + CHIPS) % CHIPS, (chip + 2) % CHIPS
    at = lambda s, c, k=core: (s, 2 * c + k)
    partner = at(slab, chip, 1 - core)
    sent = []

    def send(source, target, send_sem, recv_sem, device):
        copy = pltpu.make_async_remote_copy(
            src_ref=source, dst_ref=target, send_sem=send_sem, recv_sem=recv_sem, device_id=device, device_id_type=MESH
        )
        copy.start()
        sent.append(copy)

    def arrived(target, recv_sem):
        pltpu.make_async_copy(target, target, recv_sem).wait()

    barrier = pltpu.get_barrier_semaphore()
    other = 1 - core
    senders = (
        at(slab, behind), at(slab, behind, other), at(slab, ahead, other), partner,
        at(above, chip), at(above, chip, other), at(above, behind, other),
    )
    for device in senders:
        pl.semaphore_signal(barrier, inc=1, device_id=device, device_id_type=MESH)

    slot_chips = (ahead, across, chip, behind)

    def green_rows(slot, k):
        owner = k if slot in (FAR_A, FAR_B) else 1 - k
        return green.at[0, :, pl.ds(pl.multiple_of(512 * slot_chips[slot] + 256 * owner, 256), 256), :]

    local = []
    for slot in range(CHIPS):
        copy = pltpu.make_async_copy(green_rows(slot, core), staged.at[0, slot], green_local_sem.at[slot])
        copy.start()
        local.append(copy)

    pl.semaphore_wait(barrier, len(senders))
    for group in range(GROUPS):
        send(
            traces.at[0, :, pl.ds(32 * group, 32), :], incoming.at[group],
            first_send_sem.at[group], first_recv_sem.at[group], at(below, chip),
        )
    for slot in range(CHIPS):
        send(
            green_rows(slot, 1 - core), staged.at[1, slot], green_send_sem.at[slot], green_recv_sem.at[slot], partner
        )
    send(sources.at[0], source_block, source_send_sem, source_recv_sem, partner)

    def convert(origin, slot):
        for part in range(2):
            for half in range(2):
                high, low = split(staged[origin, slot, part, pl.ds(128 * half, 128), :])
                columns = pl.ds(256 * ((origin * 2 + part) * 2 + half), 256)
                left[slot, pl.ds(0, 128), columns] = high
                left[slot, pl.ds(128, 128), columns] = low

    for slot in range(CHIPS):
        local[slot].wait()
        convert(0, slot)
    for slot in range(CHIPS):
        arrived(staged.at[1, slot], green_recv_sem.at[slot])
        convert(1, slot)
    arrived(source_block, source_recv_sem)

    def share(step, group, value):
        value = jnp.where(slab == 0, jnp.zeros_like(value), value)
        held[step, group] = value
        send(
            held.at[step, group], partner_held.at[step, group],
            share_send_sem.at[step, group], share_recv_sem.at[step, group], partner,
        )

    lane = lax.broadcasted_iota(jnp.int32, (128, 128), 1)
    low_lanes = lane < 64
    real_lanes = lane % 64 < 32

    def make_right(step, group, origin):
        value = (held if origin == 0 else partner_held)[step, group]
        turned = jnp.where(real_lanes, -pltpu.roll(value, 96, 1), pltpu.roll(value, 32, 1))
        for part, term in ((0, value), (1, turned)):
            swapped = pltpu.roll(term, 64, 1)
            quarters = (
                jnp.where(low_lanes, term, 0.0), jnp.where(low_lanes, swapped, 0.0),
                jnp.where(low_lanes, 0.0, swapped), jnp.where(low_lanes, 0.0, term),
            )
            for index, quarter in enumerate(quarters):
                high, low = split(quarter)
                rows = pl.ds(256 * ((origin * 2 + part) * 2) + 128 * index, 128)
                right[group, rows, pl.ds(0, 128)] = high
                right[group, rows, pl.ds(128, 128)] = low

    def product(group, slot, depth=slice(None)):
        full = jnp.dot(left[slot, :, depth], right[group, depth, :], preferred_element_type=F32)
        return (full[:128, :128] + full[:128, 128:]) + (full[128:, :128] + full[128:, 128:])

    def begin(step, group):
        make_right(step, group, 0)
        for slot in (FAR_A, FAR_B) if step < STEPS - 1 else (FAR_B,):
            begun[group, slot] = product(group, slot, slice(0, 1024))

    def send_far(step, group):
        arrived(partner_held.at[step, group], share_recv_sem.at[step, group])
        make_right(step, group, 1)
        if step == STEPS - 1:
            last_products(group)
            return
        for slot, device in ((FAR_A, at(slab, ahead, other)), (FAR_B, at(slab, behind, other))):
            far_out[step, group, slot] = begun[group, slot] + product(group, slot, slice(1024, 2048))
            for piece in range(PIECES):
                rows = pl.ds(PIECE * piece, PIECE)
                send(
                    far_out.at[step, group, slot, rows], far_in.at[step, group, slot, rows],
                    far_send_sem.at[step, group, slot, piece], far_recv_sem.at[step, group, slot, piece], device,
                )

    def near_products(step, group):
        if step == STEPS - 1:
            last_near_products(group)
            return
        near_own[group, 0] = product(group, NEAR_A) + pack(source_block, group)
        near_own[group, 1] = product(group, NEAR_B)

    def send_near(step, group):
        for piece in range(PIECES):
            rows = pl.ds(PIECE * piece, PIECE)
            for side, device in ((0, at(below, chip, other)), (1, at(below, behind, other))):
                arrived(far_in.at[step, group, side, rows], far_recv_sem.at[step, group, side, piece])
                near_out[step, group, side, rows] = near_own[group, side, rows] + far_in[step, group, side, rows]
                send(
                    near_out.at[step, group, side, rows], near_in.at[step, group, side, rows],
                    near_send_sem.at[step, group, side, piece], near_recv_sem.at[step, group, side, piece], device,
                )

    def take_near(step, group):
        for piece in range(PIECES):
            for side in range(2):
                rows = pl.ds(PIECE * piece, PIECE)
                arrived(near_in.at[step, group, side, rows], near_recv_sem.at[step, group, side, piece])
        share(step + 1, group, near_in[step, group, 0] + near_in[step, group, 1])

    def send_last(group, which, device):
        send(
            last_out.at[group, which], last_in.at[group, which],
            last_send_sem.at[group, which], last_recv_sem.at[group, which], device,
        )

    def last_products(group):
        forward, backward = at(slab, ahead), at(slab, behind, other)
        far = begun[group, FAR_B] + product(group, FAR_B, slice(1024, 2048))
        last_out[group, LAST_FAR_A] = far[:64]
        send_last(group, LAST_FAR_A, forward)
        last_out[group, LAST_FAR_B] = far[64:]
        send_last(group, LAST_FAR_B, backward)
        near = product(group, FAR_A)
        last_out[group, LAST_DIRECT_A] = near[64:]
        send_last(group, LAST_DIRECT_A, forward)
        last_own[group, pl.ds(0, 64)] = near[:64]
        near = product(group, NEAR_B)
        last_out[group, LAST_DIRECT_B] = near[:64]
        send_last(group, LAST_DIRECT_B, backward)
        last_own[group, pl.ds(64, 64)] = near[64:]

    def last_near_products(group):
        last_near_out[group] = product(group, NEAR_A) + pack(source_block, group)
        send(
            last_near_out.at[group], last_near_in.at[group],
            last_near_send_sem.at[group], last_near_recv_sem.at[group], partner,
        )

    def last_relay(group):
        for side, device in ((0, at(slab, ahead)), (1, at(slab, behind, other))):
            far, out = LAST_FAR_A + side, LAST_SUM_A + side
            arrived(last_in.at[group, far], last_recv_sem.at[group, far])
            last_out[group, out] = last_own[group, pl.ds(64 * side, 64)] + last_in[group, far]
            send_last(group, out, device)

    def last_take(group):
        arrived(last_near_in.at[group], last_near_recv_sem.at[group])
        for which in (LAST_DIRECT_A, LAST_DIRECT_B, LAST_SUM_A, LAST_SUM_B):
            arrived(last_in.at[group, which], last_recv_sem.at[group, which])
        top = last_near_in[group, pl.ds(0, 64)] + (last_in[group, LAST_SUM_A] + last_in[group, LAST_DIRECT_B])
        bottom = last_near_in[group, pl.ds(64, 64)] + (last_in[group, LAST_SUM_B] + last_in[group, LAST_DIRECT_A])
        rows = jnp.concatenate([top, bottom], 0).T
        for half in range(2):
            for part in range(2):
                swept[0, part, pl.ds(32 * group, 32), pl.ds(128 * half, 128)] = rows[32 * (2 * half + part) :][:32]

    def relay(step, group):
        last_relay(group) if step == STEPS - 1 else send_near(step, group)

    def take(step, group):
        last_take(group) if step == STEPS - 1 else take_near(step, group)

    for group in range(GROUPS):
        arrived(incoming.at[group], first_recv_sem.at[group])
        share(0, group, pack(incoming.at[group], 0))
        begin(0, group)
    send_far(0, 0)
    send_far(0, 1)
    for step in range(STEPS):
        for group in range(GROUPS):
            near_products(step, group)
        for group in range(GROUPS):
            relay(step, group)
        for group in range(GROUPS):
            take(step, group)
            if step + 1 < STEPS:
                begin(step + 1, group)
                send_far(step + 1, group)
    for copy in sent:
        copy.wait_send()


def sweep(green_blocks, traces, sources):
    steps, dma = STEPS - 1, pltpu.SemaphoreType.DMA
    return pl.pallas_call(
        kernel,
        out_shape=jax.ShapeDtypeStruct(traces.shape, F32),
        in_specs=[pl.BlockSpec(memory_space=pltpu.HBM)] * 3,
        out_specs=pl.BlockSpec(memory_space=pltpu.VMEM),
        scratch_shapes=[
            pltpu.VMEM((2, CHIPS, 2, 256, 256), F32),
            pltpu.VMEM((CHIPS, 256, 2048), BF16),
            pltpu.VMEM((GROUPS, 2048, 256), BF16),
            pltpu.VMEM((2, 64, 256), F32),
            pltpu.VMEM((GROUPS, 2, 32, 256), F32),
            pltpu.VMEM((STEPS, GROUPS, 128, 128), F32),
            pltpu.VMEM((STEPS, GROUPS, 128, 128), F32),
            pltpu.VMEM((GROUPS, 2, 128, 128), F32),
            pltpu.VMEM((steps, GROUPS, 2, 128, 128), F32),
            pltpu.VMEM((steps, GROUPS, 2, 128, 128), F32),
            pltpu.VMEM((GROUPS, 2, 128, 128), F32),
            pltpu.VMEM((steps, GROUPS, 2, 128, 128), F32),
            pltpu.VMEM((steps, GROUPS, 2, 128, 128), F32),
            pltpu.VMEM((GROUPS, 128, 128), F32),
            pltpu.VMEM((GROUPS, 6, 64, 128), F32),
            pltpu.VMEM((GROUPS, 6, 64, 128), F32),
            pltpu.VMEM((GROUPS, 128, 128), F32),
            pltpu.VMEM((GROUPS, 128, 128), F32),
            dma((CHIPS,)), dma((CHIPS,)), dma((CHIPS,)), dma, dma, dma((GROUPS,)), dma((GROUPS,)),
            dma((STEPS, GROUPS)), dma((STEPS, GROUPS)),
            dma((steps, GROUPS, 2, PIECES)), dma((steps, GROUPS, 2, PIECES)),
            dma((steps, GROUPS, 2, PIECES)), dma((steps, GROUPS, 2, PIECES)),
            dma((GROUPS, 6)), dma((GROUPS, 6)), dma((GROUPS,)), dma((GROUPS,)),
        ],
        compiler_params=pltpu.CompilerParams(
            collective_id=0, has_side_effects=True, vmem_limit_bytes=67043328
        ),
        name="sweep",
    )(green_blocks, traces, sources)


def solution(mesh):
    placed = P("slab", None, None, "col")
    return jax.shard_map(sweep, mesh=mesh, in_specs=(placed,) * 3, out_specs=placed, check_vma=False)
```

```python
import jax
import jax.numpy as jnp
from jax import lax
from jax.experimental import pallas as pl
from jax.experimental.pallas import tpu as pltpu
from jax.sharding import PartitionSpec as P

STEPS = 4
GROUPS = 2
CHIPS = 4
PIECES = 2
PIECE = 128 // PIECES
MESH = pl.DeviceIdType.MESH
F32 = jnp.float32
BF16 = jnp.bfloat16

FAR_A, FAR_B, NEAR_A, NEAR_B = range(4)
LAST_FAR_A, LAST_FAR_B, LAST_DIRECT_A, LAST_DIRECT_B, LAST_SUM_A, LAST_SUM_B = range(6)


def pack(block, group):
    shots = pl.ds(32 * group, 32)
    rows = [block[part, shots, pl.ds(128 * half, 128)] for half in range(2) for part in range(2)]
    return jnp.concatenate(rows, 0).T


def split(value):
    high = value.astype(BF16)
    return high, (value - high.astype(F32)).astype(BF16)


def kernel(
    green, traces, sources, swept,
    staged, left, right, source_block, incoming, held, partner_held,
    begun, far_out, far_in, near_own, near_out, near_in, last_own, last_out, last_in, last_near_out, last_near_in,
    green_local_sem, green_send_sem, green_recv_sem, source_send_sem, source_recv_sem, first_send_sem, first_recv_sem,
    share_send_sem, share_recv_sem, far_send_sem, far_recv_sem, near_send_sem, near_recv_sem,
    last_send_sem, last_recv_sem, last_near_send_sem, last_near_recv_sem,
):
    slabs = lax.axis_size("slab")
    slab, col = lax.axis_index("slab"), lax.axis_index("col")
    chip, core = col // 2, col % 2
    sigma = 1 - 2 * (slab % 2)
    below, above = (slab + 1) % slabs, (slab + slabs - 1) % slabs
    ahead, behind, across = (chip + sigma + CHIPS) % CHIPS, (chip - sigma + CHIPS) % CHIPS, (chip + 2) % CHIPS
    at = lambda s, c, k=core: (s, 2 * c + k)
    partner = at(slab, chip, 1 - core)
    sent, sent_below = [], []

    def send(source, target, send_sem, recv_sem, device):
        copy = pltpu.make_async_remote_copy(
            src_ref=source, dst_ref=target, send_sem=send_sem, recv_sem=recv_sem, device_id=device, device_id_type=MESH
        )
        copy.start()
        sent.append(copy)

    is_first, is_last = slab == 0, slab == slabs - 1

    def send_below(source, target, send_sem, recv_sem, device):
        copy = pltpu.make_async_remote_copy(
            src_ref=source, dst_ref=target, send_sem=send_sem, recv_sem=recv_sem, device_id=device, device_id_type=MESH
        )
        pl.when(jnp.logical_not(is_last))(copy.start)
        sent_below.append(copy)

    def arrived(target, recv_sem):
        pltpu.make_async_copy(target, target, recv_sem).wait()

    barrier = pltpu.get_barrier_semaphore()
    other = 1 - core
    same_slab = (at(slab, behind), at(slab, behind, other), at(slab, ahead, other), partner)
    from_above = (at(above, chip), at(above, chip, other), at(above, behind, other))
    for device in same_slab:
        pl.semaphore_signal(barrier, inc=1, device_id=device, device_id_type=MESH)

    @pl.when(jnp.logical_not(is_first))
    def _():
        for device in from_above:
            pl.semaphore_signal(barrier, inc=1, device_id=device, device_id_type=MESH)

    slot_chips = (ahead, across, chip, behind)

    def green_rows(slot, k):
        owner = k if slot in (FAR_A, FAR_B) else 1 - k
        return green.at[0, :, pl.ds(pl.multiple_of(512 * slot_chips[slot] + 256 * owner, 256), 256), :]

    local = []
    for slot in range(CHIPS):
        copy = pltpu.make_async_copy(green_rows(slot, core), staged.at[0, slot], green_local_sem.at[slot])
        copy.start()
        local.append(copy)

    @pl.when(is_last)
    def _():
        pl.semaphore_wait(barrier, len(same_slab))

    @pl.when(jnp.logical_not(is_last))
    def _():
        pl.semaphore_wait(barrier, len(same_slab) + len(from_above))

    for group in range(GROUPS):
        send_below(
            traces.at[0, :, pl.ds(32 * group, 32), :], incoming.at[group],
            first_send_sem.at[group], first_recv_sem.at[group], at(below, chip),
        )
    for slot in range(CHIPS):
        send(
            green_rows(slot, 1 - core), staged.at[1, slot], green_send_sem.at[slot], green_recv_sem.at[slot], partner
        )
    send(sources.at[0], source_block, source_send_sem, source_recv_sem, partner)

    def convert(origin, slot):
        for part in range(2):
            for half in range(2):
                high, low = split(staged[origin, slot, part, pl.ds(128 * half, 128), :])
                columns = pl.ds(256 * ((origin * 2 + part) * 2 + half), 256)
                left[slot, pl.ds(0, 128), columns] = high
                left[slot, pl.ds(128, 128), columns] = low

    for slot in range(CHIPS):
        local[slot].wait()
        convert(0, slot)
    for slot in range(CHIPS):
        arrived(staged.at[1, slot], green_recv_sem.at[slot])
        convert(1, slot)
    arrived(source_block, source_recv_sem)

    def share(step, group, value_of):
        @pl.when(is_first)
        def _():
            held[step, group] = jnp.zeros((128, 128), F32)

        @pl.when(jnp.logical_not(is_first))
        def _():
            held[step, group] = value_of()

        send(
            held.at[step, group], partner_held.at[step, group],
            share_send_sem.at[step, group], share_recv_sem.at[step, group], partner,
        )

    lane = lax.broadcasted_iota(jnp.int32, (128, 128), 1)
    low_lanes = lane < 64
    real_lanes = lane % 64 < 32

    def make_right(step, group, origin):
        value = (held if origin == 0 else partner_held)[step, group]
        turned = jnp.where(real_lanes, -pltpu.roll(value, 96, 1), pltpu.roll(value, 32, 1))
        for part, term in ((0, value), (1, turned)):
            swapped = pltpu.roll(term, 64, 1)
            quarters = (
                jnp.where(low_lanes, term, 0.0), jnp.where(low_lanes, swapped, 0.0),
                jnp.where(low_lanes, 0.0, swapped), jnp.where(low_lanes, 0.0, term),
            )
            for index, quarter in enumerate(quarters):
                high, low = split(quarter)
                rows = pl.ds(256 * ((origin * 2 + part) * 2) + 128 * index, 128)
                right[group, rows, pl.ds(0, 128)] = high
                right[group, rows, pl.ds(128, 128)] = low

    def product(group, slot, depth=slice(None)):
        full = jnp.dot(left[slot, :, depth], right[group, depth, :], preferred_element_type=F32)
        return (full[:128, :128] + full[:128, 128:]) + (full[128:, :128] + full[128:, 128:])

    def begin(step, group):
        make_right(step, group, 0)
        for slot in (FAR_A, FAR_B) if step < STEPS - 1 else (FAR_B,):
            begun[group, slot] = product(group, slot, slice(0, 1024))

    def send_far(step, group):
        arrived(partner_held.at[step, group], share_recv_sem.at[step, group])
        make_right(step, group, 1)
        if step == STEPS - 1:
            last_products(group)
            return
        for slot, device in ((FAR_A, at(slab, ahead, other)), (FAR_B, at(slab, behind, other))):
            far_out[step, group, slot] = begun[group, slot] + product(group, slot, slice(1024, 2048))
            for piece in range(PIECES):
                rows = pl.ds(PIECE * piece, PIECE)
                send(
                    far_out.at[step, group, slot, rows], far_in.at[step, group, slot, rows],
                    far_send_sem.at[step, group, slot, piece], far_recv_sem.at[step, group, slot, piece], device,
                )

    def near_products(step, group):
        if step == STEPS - 1:
            last_near_products(group)
            return
        near_own[group, 0] = product(group, NEAR_A) + pack(source_block, group)
        near_own[group, 1] = product(group, NEAR_B)

    def send_near(step, group):
        for piece in range(PIECES):
            rows = pl.ds(PIECE * piece, PIECE)
            for side, device in ((0, at(below, chip, other)), (1, at(below, behind, other))):
                arrived(far_in.at[step, group, side, rows], far_recv_sem.at[step, group, side, piece])
                near_out[step, group, side, rows] = near_own[group, side, rows] + far_in[step, group, side, rows]
                send_below(
                    near_out.at[step, group, side, rows], near_in.at[step, group, side, rows],
                    near_send_sem.at[step, group, side, piece], near_recv_sem.at[step, group, side, piece], device,
                )

    def take_near(step, group):
        def value_of():
            for piece in range(PIECES):
                for side in range(2):
                    rows = pl.ds(PIECE * piece, PIECE)
                    arrived(near_in.at[step, group, side, rows], near_recv_sem.at[step, group, side, piece])
            return near_in[step, group, 0] + near_in[step, group, 1]

        share(step + 1, group, value_of)

    def take_first(group):
        def value_of():
            arrived(incoming.at[group], first_recv_sem.at[group])
            return pack(incoming.at[group], 0)

        share(0, group, value_of)

    def send_last(group, which, device):
        send(
            last_out.at[group, which], last_in.at[group, which],
            last_send_sem.at[group, which], last_recv_sem.at[group, which], device,
        )

    def last_products(group):
        forward, backward = at(slab, ahead), at(slab, behind, other)
        far = begun[group, FAR_B] + product(group, FAR_B, slice(1024, 2048))
        last_out[group, LAST_FAR_A] = far[:64]
        send_last(group, LAST_FAR_A, forward)
        last_out[group, LAST_FAR_B] = far[64:]
        send_last(group, LAST_FAR_B, backward)
        near = product(group, FAR_A)
        last_out[group, LAST_DIRECT_A] = near[64:]
        send_last(group, LAST_DIRECT_A, forward)
        last_own[group, pl.ds(0, 64)] = near[:64]
        near = product(group, NEAR_B)
        last_out[group, LAST_DIRECT_B] = near[:64]
        send_last(group, LAST_DIRECT_B, backward)
        last_own[group, pl.ds(64, 64)] = near[64:]

    def last_near_products(group):
        last_near_out[group] = product(group, NEAR_A) + pack(source_block, group)
        send(
            last_near_out.at[group], last_near_in.at[group],
            last_near_send_sem.at[group], last_near_recv_sem.at[group], partner,
        )

    def last_relay(group):
        for side, device in ((0, at(slab, ahead)), (1, at(slab, behind, other))):
            far, out = LAST_FAR_A + side, LAST_SUM_A + side
            arrived(last_in.at[group, far], last_recv_sem.at[group, far])
            last_out[group, out] = last_own[group, pl.ds(64 * side, 64)] + last_in[group, far]
            send_last(group, out, device)

    def last_take(group):
        arrived(last_near_in.at[group], last_near_recv_sem.at[group])
        for which in (LAST_DIRECT_A, LAST_DIRECT_B, LAST_SUM_A, LAST_SUM_B):
            arrived(last_in.at[group, which], last_recv_sem.at[group, which])
        top = last_near_in[group, pl.ds(0, 64)] + (last_in[group, LAST_SUM_A] + last_in[group, LAST_DIRECT_B])
        bottom = last_near_in[group, pl.ds(64, 64)] + (last_in[group, LAST_SUM_B] + last_in[group, LAST_DIRECT_A])
        rows = jnp.concatenate([top, bottom], 0).T
        for half in range(2):
            for part in range(2):
                swept[0, part, pl.ds(32 * group, 32), pl.ds(128 * half, 128)] = rows[32 * (2 * half + part) :][:32]

    def relay(step, group):
        last_relay(group) if step == STEPS - 1 else send_near(step, group)

    def take(step, group):
        last_take(group) if step == STEPS - 1 else take_near(step, group)

    for group in range(GROUPS):
        take_first(group)
        begin(0, group)
    send_far(0, 0)
    send_far(0, 1)
    for step in range(STEPS):
        for group in range(GROUPS):
            near_products(step, group)
        for group in range(GROUPS):
            relay(step, group)
        for group in range(GROUPS):
            take(step, group)
            if step + 1 < STEPS:
                begin(step + 1, group)
                send_far(step + 1, group)
    for copy in sent:
        copy.wait_send()

    @pl.when(jnp.logical_not(is_last))
    def _():
        for copy in sent_below:
            copy.wait_send()


def sweep(green_blocks, traces, sources):
    steps, dma = STEPS - 1, pltpu.SemaphoreType.DMA
    return pl.pallas_call(
        kernel,
        out_shape=jax.ShapeDtypeStruct(traces.shape, F32),
        in_specs=[pl.BlockSpec(memory_space=pltpu.HBM)] * 3,
        out_specs=pl.BlockSpec(memory_space=pltpu.VMEM),
        scratch_shapes=[
            pltpu.VMEM((2, CHIPS, 2, 256, 256), F32),
            pltpu.VMEM((CHIPS, 256, 2048), BF16),
            pltpu.VMEM((GROUPS, 2048, 256), BF16),
            pltpu.VMEM((2, 64, 256), F32),
            pltpu.VMEM((GROUPS, 2, 32, 256), F32),
            pltpu.VMEM((STEPS, GROUPS, 128, 128), F32),
            pltpu.VMEM((STEPS, GROUPS, 128, 128), F32),
            pltpu.VMEM((GROUPS, 2, 128, 128), F32),
            pltpu.VMEM((steps, GROUPS, 2, 128, 128), F32),
            pltpu.VMEM((steps, GROUPS, 2, 128, 128), F32),
            pltpu.VMEM((GROUPS, 2, 128, 128), F32),
            pltpu.VMEM((steps, GROUPS, 2, 128, 128), F32),
            pltpu.VMEM((steps, GROUPS, 2, 128, 128), F32),
            pltpu.VMEM((GROUPS, 128, 128), F32),
            pltpu.VMEM((GROUPS, 6, 64, 128), F32),
            pltpu.VMEM((GROUPS, 6, 64, 128), F32),
            pltpu.VMEM((GROUPS, 128, 128), F32),
            pltpu.VMEM((GROUPS, 128, 128), F32),
            dma((CHIPS,)), dma((CHIPS,)), dma((CHIPS,)), dma, dma, dma((GROUPS,)), dma((GROUPS,)),
            dma((STEPS, GROUPS)), dma((STEPS, GROUPS)),
            dma((steps, GROUPS, 2, PIECES)), dma((steps, GROUPS, 2, PIECES)),
            dma((steps, GROUPS, 2, PIECES)), dma((steps, GROUPS, 2, PIECES)),
            dma((GROUPS, 6)), dma((GROUPS, 6)), dma((GROUPS,)), dma((GROUPS,)),
        ],
        compiler_params=pltpu.CompilerParams(
            collective_id=0, has_side_effects=True, vmem_limit_bytes=67043328
        ),
        name="sweep",
    )(green_blocks, traces, sources)


def solution(mesh):
    placed = P("slab", None, None, "col")
    return jax.shard_map(sweep, mesh=mesh, in_specs=(placed,) * 3, out_specs=placed, check_vma=False)
```

```python
import jax
import jax.numpy as jnp
from jax import lax
from jax.experimental import pallas as pl
from jax.experimental.pallas import tpu as pltpu
from jax.sharding import PartitionSpec as P

STEPS = 4
GROUPS = 2
CHIPS = 4
PIECES = 2
PIECE = 128 // PIECES
MESH = pl.DeviceIdType.MESH
F32 = jnp.float32
BF16 = jnp.bfloat16

FAR_A, FAR_B, NEAR_A, NEAR_B = range(4)
LAST_FAR_A, LAST_FAR_B, LAST_DIRECT_A, LAST_DIRECT_B, LAST_SUM_A, LAST_SUM_B = range(6)


def pack(block, group):
    shots = pl.ds(32 * group, 32)
    rows = [block[part, shots, pl.ds(128 * half, 128)] for half in range(2) for part in range(2)]
    return jnp.concatenate(rows, 0).T


def split(value):
    high = value.astype(BF16)
    return high, (value - high.astype(F32)).astype(BF16)


def kernel(
    green, traces, sources, swept,
    staged, left, right, source_block, incoming, held, partner_held,
    begun, far_out, far_in, near_own, near_out, near_in, last_own, last_out, last_in, last_near_out, last_near_in,
    green_local_sem, green_send_sem, green_recv_sem, source_send_sem, source_recv_sem, first_send_sem, first_recv_sem,
    share_send_sem, share_recv_sem, far_send_sem, far_recv_sem, near_send_sem, near_recv_sem,
    last_send_sem, last_recv_sem, last_near_send_sem, last_near_recv_sem,
):
    slabs = lax.axis_size("slab")
    slab, col = lax.axis_index("slab"), lax.axis_index("col")
    chip, core = col // 2, col % 2
    sigma = 1 - 2 * (slab % 2)
    below, above = (slab + 1) % slabs, (slab + slabs - 1) % slabs
    ahead, behind, across = (chip + sigma + CHIPS) % CHIPS, (chip - sigma + CHIPS) % CHIPS, (chip + 2) % CHIPS
    at = lambda s, c, k=core: (s, 2 * c + k)
    partner = at(slab, chip, 1 - core)
    sent, sent_below = [], []

    def send(source, target, send_sem, recv_sem, device):
        copy = pltpu.make_async_remote_copy(
            src_ref=source, dst_ref=target, send_sem=send_sem, recv_sem=recv_sem, device_id=device, device_id_type=MESH
        )
        copy.start()
        sent.append(copy)

    is_first, is_last = slab == 0, slab == slabs - 1

    def send_below(source, target, send_sem, recv_sem, device):
        copy = pltpu.make_async_remote_copy(
            src_ref=source, dst_ref=target, send_sem=send_sem, recv_sem=recv_sem, device_id=device, device_id_type=MESH
        )
        pl.when(jnp.logical_not(is_last))(copy.start)
        sent_below.append(copy)

    def arrived(target, recv_sem):
        pltpu.make_async_copy(target, target, recv_sem).wait()

    barrier = pltpu.get_barrier_semaphore()
    other = 1 - core
    same_slab = (at(slab, behind), at(slab, behind, other), at(slab, ahead, other), partner)
    from_above = (at(above, chip), at(above, chip, other), at(above, behind, other))
    for device in same_slab:
        pl.semaphore_signal(barrier, inc=1, device_id=device, device_id_type=MESH)

    @pl.when(jnp.logical_not(is_first))
    def _():
        for device in from_above:
            pl.semaphore_signal(barrier, inc=1, device_id=device, device_id_type=MESH)

    slot_chips = (ahead, across, chip, behind)

    def green_rows(slot, k):
        owner = k if slot in (FAR_A, FAR_B) else 1 - k
        return green.at[0, :, pl.ds(pl.multiple_of(512 * slot_chips[slot] + 256 * owner, 256), 256), :]

    local = []
    for slot in range(CHIPS):
        copy = pltpu.make_async_copy(green_rows(slot, core), staged.at[0, slot], green_local_sem.at[slot])
        copy.start()
        local.append(copy)

    @pl.when(is_last)
    def _():
        pl.semaphore_wait(barrier, len(same_slab))

    @pl.when(jnp.logical_not(is_last))
    def _():
        pl.semaphore_wait(barrier, len(same_slab) + len(from_above))

    for group in range(GROUPS):
        send_below(
            traces.at[0, :, pl.ds(32 * group, 32), :], incoming.at[group],
            first_send_sem.at[group], first_recv_sem.at[group], at(below, chip),
        )
    for slot in range(CHIPS):
        send(
            green_rows(slot, 1 - core), staged.at[1, slot], green_send_sem.at[slot], green_recv_sem.at[slot], partner
        )
    send(sources.at[0], source_block, source_send_sem, source_recv_sem, partner)

    def convert(origin, slot):
        for part in range(2):
            high, low = split(staged[origin, slot, part])
            columns = pl.ds(256 * (origin * 2 + part), 256)
            left[slot, pl.ds(0, 256), columns] = high
            left[slot, pl.ds(256, 256), columns] = low

    for slot in range(CHIPS):
        local[slot].wait()
        convert(0, slot)
    for slot in range(CHIPS):
        arrived(staged.at[1, slot], green_recv_sem.at[slot])
        convert(1, slot)
    arrived(source_block, source_recv_sem)

    def share(step, group, value_of):
        @pl.when(is_first)
        def _():
            held[step, group] = jnp.zeros((128, 128), F32)

        @pl.when(jnp.logical_not(is_first))
        def _():
            held[step, group] = value_of()

        send(
            held.at[step, group], partner_held.at[step, group],
            share_send_sem.at[step, group], share_recv_sem.at[step, group], partner,
        )

    lane = lax.broadcasted_iota(jnp.int32, (128, 128), 1)
    low_lanes = lane < 64
    real_lanes = lane % 64 < 32

    def make_right(step, group, origin):
        value = (held if origin == 0 else partner_held)[step, group]
        turned = jnp.where(real_lanes, -pltpu.roll(value, 96, 1), pltpu.roll(value, 32, 1))
        for part, term in ((0, value), (1, turned)):
            high = term.astype(BF16).astype(F32)
            low = term - high
            rows = 256 * (origin * 2 + part)
            first = jnp.where(low_lanes, high, pltpu.roll(low, 64, 1))
            second = jnp.where(low_lanes, pltpu.roll(high, 64, 1), low)
            right[group, pl.ds(rows, 128), :] = first.astype(BF16)
            right[group, pl.ds(rows + 128, 128), :] = second.astype(BF16)

    def product(group, slot, depth=slice(None)):
        full = jnp.dot(left[slot, :, depth], right[group, depth, :], preferred_element_type=F32)
        full = full[:256] + full[256:]
        full = full + pltpu.roll(full, 64, 1)
        return jnp.where(low_lanes, full[:128], full[128:])

    def begin(step, group):
        make_right(step, group, 0)
        for slot in (FAR_A, FAR_B) if step < STEPS - 1 else (FAR_B,):
            begun[group, slot] = product(group, slot, slice(0, 512))

    def send_far(step, group):
        arrived(partner_held.at[step, group], share_recv_sem.at[step, group])
        make_right(step, group, 1)
        if step == STEPS - 1:
            last_products(group)
            return
        for slot, device in ((FAR_A, at(slab, ahead, other)), (FAR_B, at(slab, behind, other))):
            far_out[step, group, slot] = begun[group, slot] + product(group, slot, slice(512, 1024))
            for piece in range(PIECES):
                rows = pl.ds(PIECE * piece, PIECE)
                send(
                    far_out.at[step, group, slot, rows], far_in.at[step, group, slot, rows],
                    far_send_sem.at[step, group, slot, piece], far_recv_sem.at[step, group, slot, piece], device,
                )

    def near_products(step, group):
        if step == STEPS - 1:
            last_near_products(group)
            return
        near_own[group, 0] = product(group, NEAR_A) + pack(source_block, group)
        near_own[group, 1] = product(group, NEAR_B)

    def send_near(step, group):
        for piece in range(PIECES):
            rows = pl.ds(PIECE * piece, PIECE)
            for side, device in ((0, at(below, chip, other)), (1, at(below, behind, other))):
                arrived(far_in.at[step, group, side, rows], far_recv_sem.at[step, group, side, piece])
                near_out[step, group, side, rows] = near_own[group, side, rows] + far_in[step, group, side, rows]
                send_below(
                    near_out.at[step, group, side, rows], near_in.at[step, group, side, rows],
                    near_send_sem.at[step, group, side, piece], near_recv_sem.at[step, group, side, piece], device,
                )

    def take_near(step, group):
        def value_of():
            for piece in range(PIECES):
                for side in range(2):
                    rows = pl.ds(PIECE * piece, PIECE)
                    arrived(near_in.at[step, group, side, rows], near_recv_sem.at[step, group, side, piece])
            return near_in[step, group, 0] + near_in[step, group, 1]

        share(step + 1, group, value_of)

    def take_first(group):
        def value_of():
            arrived(incoming.at[group], first_recv_sem.at[group])
            return pack(incoming.at[group], 0)

        share(0, group, value_of)

    def send_last(group, which, device):
        send(
            last_out.at[group, which], last_in.at[group, which],
            last_send_sem.at[group, which], last_recv_sem.at[group, which], device,
        )

    def last_products(group):
        forward, backward = at(slab, ahead), at(slab, behind, other)
        far = begun[group, FAR_B] + product(group, FAR_B, slice(512, 1024))
        last_out[group, LAST_FAR_A] = far[:64]
        send_last(group, LAST_FAR_A, forward)
        last_out[group, LAST_FAR_B] = far[64:]
        send_last(group, LAST_FAR_B, backward)
        near = product(group, FAR_A)
        last_out[group, LAST_DIRECT_A] = near[64:]
        send_last(group, LAST_DIRECT_A, forward)
        last_own[group, pl.ds(0, 64)] = near[:64]
        near = product(group, NEAR_B)
        last_out[group, LAST_DIRECT_B] = near[:64]
        send_last(group, LAST_DIRECT_B, backward)
        last_own[group, pl.ds(64, 64)] = near[64:]

    def last_near_products(group):
        last_near_out[group] = product(group, NEAR_A) + pack(source_block, group)
        send(
            last_near_out.at[group], last_near_in.at[group],
            last_near_send_sem.at[group], last_near_recv_sem.at[group], partner,
        )

    def last_relay(group):
        for side, device in ((0, at(slab, ahead)), (1, at(slab, behind, other))):
            far, out = LAST_FAR_A + side, LAST_SUM_A + side
            arrived(last_in.at[group, far], last_recv_sem.at[group, far])
            last_out[group, out] = last_own[group, pl.ds(64 * side, 64)] + last_in[group, far]
            send_last(group, out, device)

    def last_take(group):
        arrived(last_near_in.at[group], last_near_recv_sem.at[group])
        for which in (LAST_DIRECT_A, LAST_DIRECT_B, LAST_SUM_A, LAST_SUM_B):
            arrived(last_in.at[group, which], last_recv_sem.at[group, which])
        top = last_near_in[group, pl.ds(0, 64)] + (last_in[group, LAST_SUM_A] + last_in[group, LAST_DIRECT_B])
        bottom = last_near_in[group, pl.ds(64, 64)] + (last_in[group, LAST_SUM_B] + last_in[group, LAST_DIRECT_A])
        rows = jnp.concatenate([top, bottom], 0).T
        for half in range(2):
            for part in range(2):
                swept[0, part, pl.ds(32 * group, 32), pl.ds(128 * half, 128)] = rows[32 * (2 * half + part) :][:32]

    def relay(step, group):
        last_relay(group) if step == STEPS - 1 else send_near(step, group)

    def take(step, group):
        last_take(group) if step == STEPS - 1 else take_near(step, group)

    for group in range(GROUPS):
        take_first(group)
        begin(0, group)
    send_far(0, 0)
    send_far(0, 1)
    for step in range(STEPS):
        for group in range(GROUPS):
            near_products(step, group)
        for group in range(GROUPS):
            relay(step, group)
        for group in range(GROUPS):
            take(step, group)
            if step + 1 < STEPS:
                begin(step + 1, group)
                send_far(step + 1, group)
    for copy in sent:
        copy.wait_send()

    @pl.when(jnp.logical_not(is_last))
    def _():
        for copy in sent_below:
            copy.wait_send()


def sweep(green_blocks, traces, sources):
    steps, dma = STEPS - 1, pltpu.SemaphoreType.DMA
    return pl.pallas_call(
        kernel,
        out_shape=jax.ShapeDtypeStruct(traces.shape, F32),
        in_specs=[pl.BlockSpec(memory_space=pltpu.HBM)] * 3,
        out_specs=pl.BlockSpec(memory_space=pltpu.VMEM),
        scratch_shapes=[
            pltpu.VMEM((2, CHIPS, 2, 256, 256), F32),
            pltpu.VMEM((CHIPS, 512, 1024), BF16),
            pltpu.VMEM((GROUPS, 1024, 128), BF16),
            pltpu.VMEM((2, 64, 256), F32),
            pltpu.VMEM((GROUPS, 2, 32, 256), F32),
            pltpu.VMEM((STEPS, GROUPS, 128, 128), F32),
            pltpu.VMEM((STEPS, GROUPS, 128, 128), F32),
            pltpu.VMEM((GROUPS, 2, 128, 128), F32),
            pltpu.VMEM((steps, GROUPS, 2, 128, 128), F32),
            pltpu.VMEM((steps, GROUPS, 2, 128, 128), F32),
            pltpu.VMEM((GROUPS, 2, 128, 128), F32),
            pltpu.VMEM((steps, GROUPS, 2, 128, 128), F32),
            pltpu.VMEM((steps, GROUPS, 2, 128, 128), F32),
            pltpu.VMEM((GROUPS, 128, 128), F32),
            pltpu.VMEM((GROUPS, 6, 64, 128), F32),
            pltpu.VMEM((GROUPS, 6, 64, 128), F32),
            pltpu.VMEM((GROUPS, 128, 128), F32),
            pltpu.VMEM((GROUPS, 128, 128), F32),
            dma((CHIPS,)), dma((CHIPS,)), dma((CHIPS,)), dma, dma, dma((GROUPS,)), dma((GROUPS,)),
            dma((STEPS, GROUPS)), dma((STEPS, GROUPS)),
            dma((steps, GROUPS, 2, PIECES)), dma((steps, GROUPS, 2, PIECES)),
            dma((steps, GROUPS, 2, PIECES)), dma((steps, GROUPS, 2, PIECES)),
            dma((GROUPS, 6)), dma((GROUPS, 6)), dma((GROUPS,)), dma((GROUPS,)),
        ],
        compiler_params=pltpu.CompilerParams(
            collective_id=0, has_side_effects=True, vmem_limit_bytes=67043328
        ),
        name="sweep",
    )(green_blocks, traces, sources)


def solution(mesh):
    placed = P("slab", None, None, "col")
    return jax.shard_map(sweep, mesh=mesh, in_specs=(placed,) * 3, out_specs=placed, check_vma=False)
```

```python
import jax
import jax.numpy as jnp
from jax import lax
from jax.experimental import pallas as pl
from jax.experimental.pallas import tpu as pltpu
from jax.sharding import PartitionSpec as P

STEPS = 4
GROUPS = 2
CHIPS = 4
PIECES = 4
PIECE = 128 // PIECES
MESH = pl.DeviceIdType.MESH
F32 = jnp.float32
BF16 = jnp.bfloat16

FAR_A, FAR_B, NEAR_A, NEAR_B = range(4)
LAST_FAR_A, LAST_FAR_B, LAST_DIRECT_A, LAST_DIRECT_B, LAST_SUM_A, LAST_SUM_B = range(6)


def pack(block, group):
    shots = pl.ds(32 * group, 32)
    rows = [block[part, shots, pl.ds(128 * half, 128)] for half in range(2) for part in range(2)]
    return jnp.concatenate(rows, 0).T


def split(value):
    high = value.astype(BF16)
    return high, (value - high.astype(F32)).astype(BF16)


def kernel(
    green, traces, sources, swept,
    staged, left, right, source_block, incoming, held, partner_held,
    begun, far_out, far_in, near_own, near_out, near_in, last_own, last_out, last_in, last_near_out, last_near_in,
    green_local_sem, green_send_sem, green_recv_sem, source_send_sem, source_recv_sem, first_send_sem, first_recv_sem,
    share_send_sem, share_recv_sem, far_send_sem, far_recv_sem, near_send_sem, near_recv_sem,
    last_send_sem, last_recv_sem, last_near_send_sem, last_near_recv_sem,
):
    slabs = lax.axis_size("slab")
    slab, col = lax.axis_index("slab"), lax.axis_index("col")
    chip, core = col // 2, col % 2
    sigma = 1 - 2 * (slab % 2)
    below, above = (slab + 1) % slabs, (slab + slabs - 1) % slabs
    ahead, behind, across = (chip + sigma + CHIPS) % CHIPS, (chip - sigma + CHIPS) % CHIPS, (chip + 2) % CHIPS
    at = lambda s, c, k=core: (s, 2 * c + k)
    partner = at(slab, chip, 1 - core)
    sent, sent_below = [], []

    def send(source, target, send_sem, recv_sem, device):
        copy = pltpu.make_async_remote_copy(
            src_ref=source, dst_ref=target, send_sem=send_sem, recv_sem=recv_sem, device_id=device, device_id_type=MESH
        )
        copy.start()
        sent.append(copy)

    is_first, is_last = slab == 0, slab == slabs - 1

    def send_below(source, target, send_sem, recv_sem, device):
        copy = pltpu.make_async_remote_copy(
            src_ref=source, dst_ref=target, send_sem=send_sem, recv_sem=recv_sem, device_id=device, device_id_type=MESH
        )
        pl.when(jnp.logical_not(is_last))(copy.start)
        sent_below.append(copy)

    def arrived(target, recv_sem):
        pltpu.make_async_copy(target, target, recv_sem).wait()

    barrier = pltpu.get_barrier_semaphore()
    other = 1 - core
    same_slab = (at(slab, behind), at(slab, behind, other), at(slab, ahead, other), partner)
    from_above = (at(above, chip), at(above, chip, other), at(above, behind, other))
    for device in same_slab:
        pl.semaphore_signal(barrier, inc=1, device_id=device, device_id_type=MESH)

    @pl.when(jnp.logical_not(is_first))
    def _():
        for device in from_above:
            pl.semaphore_signal(barrier, inc=1, device_id=device, device_id_type=MESH)

    slot_chips = (ahead, across, chip, behind)

    def green_rows(slot, k):
        owner = k if slot in (FAR_A, FAR_B) else 1 - k
        return green.at[0, :, pl.ds(pl.multiple_of(512 * slot_chips[slot] + 256 * owner, 256), 256), :]

    local = []
    for slot in range(CHIPS):
        copy = pltpu.make_async_copy(green_rows(slot, core), staged.at[0, slot], green_local_sem.at[slot])
        copy.start()
        local.append(copy)

    @pl.when(is_last)
    def _():
        pl.semaphore_wait(barrier, len(same_slab))

    @pl.when(jnp.logical_not(is_last))
    def _():
        pl.semaphore_wait(barrier, len(same_slab) + len(from_above))

    for group in range(GROUPS):
        send_below(
            traces.at[0, :, pl.ds(32 * group, 32), :], incoming.at[group],
            first_send_sem.at[group], first_recv_sem.at[group], at(below, chip),
        )
    for slot in range(CHIPS):
        send(
            green_rows(slot, 1 - core), staged.at[1, slot], green_send_sem.at[slot], green_recv_sem.at[slot], partner
        )
    send(sources.at[0], source_block, source_send_sem, source_recv_sem, partner)

    def convert(origin, slot):
        for part in range(2):
            for half in range(2):
                high, low = split(staged[origin, slot, part, pl.ds(128 * half, 128), :])
                columns = pl.ds(256 * ((origin * 2 + part) * 2 + half), 256)
                left[slot, pl.ds(0, 128), columns] = high
                left[slot, pl.ds(128, 128), columns] = low

    for slot in range(CHIPS):
        local[slot].wait()
        convert(0, slot)
    for slot in range(CHIPS):
        arrived(staged.at[1, slot], green_recv_sem.at[slot])
        convert(1, slot)
    arrived(source_block, source_recv_sem)

    def share(step, group, value_of):
        @pl.when(is_first)
        def _():
            held[step, group] = jnp.zeros((128, 128), F32)

        @pl.when(jnp.logical_not(is_first))
        def _():
            held[step, group] = value_of()

        send(
            held.at[step, group], partner_held.at[step, group],
            share_send_sem.at[step, group], share_recv_sem.at[step, group], partner,
        )

    lane = lax.broadcasted_iota(jnp.int32, (128, 128), 1)
    low_lanes = lane < 64
    real_lanes = lane % 64 < 32

    def make_right(step, group, origin):
        value = (held if origin == 0 else partner_held)[step, group]
        turned = jnp.where(real_lanes, -pltpu.roll(value, 96, 1), pltpu.roll(value, 32, 1))
        for part, term in ((0, value), (1, turned)):
            swapped = pltpu.roll(term, 64, 1)
            quarters = (
                jnp.where(low_lanes, term, 0.0), jnp.where(low_lanes, swapped, 0.0),
                jnp.where(low_lanes, 0.0, swapped), jnp.where(low_lanes, 0.0, term),
            )
            for index, quarter in enumerate(quarters):
                high, low = split(quarter)
                rows = pl.ds(256 * ((origin * 2 + part) * 2) + 128 * index, 128)
                right[group, rows, pl.ds(0, 128)] = high
                right[group, rows, pl.ds(128, 128)] = low

    def product(group, slot, depth=slice(None)):
        full = jnp.dot(left[slot, :, depth], right[group, depth, :], preferred_element_type=F32)
        return (full[:128, :128] + full[:128, 128:]) + (full[128:, :128] + full[128:, 128:])

    def begin(step, group):
        make_right(step, group, 0)
        for slot in (FAR_A, FAR_B) if step < STEPS - 1 else (FAR_B,):
            begun[group, slot] = product(group, slot, slice(0, 1024))

    def send_far(step, group):
        arrived(partner_held.at[step, group], share_recv_sem.at[step, group])
        make_right(step, group, 1)
        if step == STEPS - 1:
            last_products(group)
            return
        for slot, device in ((FAR_A, at(slab, ahead, other)), (FAR_B, at(slab, behind, other))):
            far_out[step, group, slot] = begun[group, slot] + product(group, slot, slice(1024, 2048))
            for piece in range(PIECES):
                rows = pl.ds(PIECE * piece, PIECE)
                send(
                    far_out.at[step, group, slot, rows], far_in.at[step, group, slot, rows],
                    far_send_sem.at[step, group, slot, piece], far_recv_sem.at[step, group, slot, piece], device,
                )

    def near_products(step, group):
        if step == STEPS - 1:
            last_near_products(group)
            return
        near_own[group, 0] = product(group, NEAR_A) + pack(source_block, group)
        near_own[group, 1] = product(group, NEAR_B)

    def send_near(step, group):
        for piece in range(PIECES):
            rows = pl.ds(PIECE * piece, PIECE)
            for side, device in ((0, at(below, chip, other)), (1, at(below, behind, other))):
                arrived(far_in.at[step, group, side, rows], far_recv_sem.at[step, group, side, piece])
                near_out[step, group, side, rows] = near_own[group, side, rows] + far_in[step, group, side, rows]
                send_below(
                    near_out.at[step, group, side, rows], near_in.at[step, group, side, rows],
                    near_send_sem.at[step, group, side, piece], near_recv_sem.at[step, group, side, piece], device,
                )

    def take_near(step, group):
        def value_of():
            for piece in range(PIECES):
                for side in range(2):
                    rows = pl.ds(PIECE * piece, PIECE)
                    arrived(near_in.at[step, group, side, rows], near_recv_sem.at[step, group, side, piece])
            return near_in[step, group, 0] + near_in[step, group, 1]

        share(step + 1, group, value_of)

    def take_first(group):
        def value_of():
            arrived(incoming.at[group], first_recv_sem.at[group])
            return pack(incoming.at[group], 0)

        share(0, group, value_of)

    def send_last(group, which, device):
        send(
            last_out.at[group, which], last_in.at[group, which],
            last_send_sem.at[group, which], last_recv_sem.at[group, which], device,
        )

    def last_products(group):
        forward, backward = at(slab, ahead), at(slab, behind, other)
        far = begun[group, FAR_B] + product(group, FAR_B, slice(1024, 2048))
        last_out[group, LAST_FAR_A] = far[:64]
        send_last(group, LAST_FAR_A, forward)
        last_out[group, LAST_FAR_B] = far[64:]
        send_last(group, LAST_FAR_B, backward)
        near = product(group, FAR_A)
        last_out[group, LAST_DIRECT_A] = near[64:]
        send_last(group, LAST_DIRECT_A, forward)
        last_own[group, pl.ds(0, 64)] = near[:64]
        near = product(group, NEAR_B)
        last_out[group, LAST_DIRECT_B] = near[:64]
        send_last(group, LAST_DIRECT_B, backward)
        last_own[group, pl.ds(64, 64)] = near[64:]

    def last_near_products(group):
        last_near_out[group] = product(group, NEAR_A) + pack(source_block, group)
        send(
            last_near_out.at[group], last_near_in.at[group],
            last_near_send_sem.at[group], last_near_recv_sem.at[group], partner,
        )

    def last_relay(group):
        for side, device in ((0, at(slab, ahead)), (1, at(slab, behind, other))):
            far, out = LAST_FAR_A + side, LAST_SUM_A + side
            arrived(last_in.at[group, far], last_recv_sem.at[group, far])
            last_out[group, out] = last_own[group, pl.ds(64 * side, 64)] + last_in[group, far]
            send_last(group, out, device)

    def last_take(group):
        arrived(last_near_in.at[group], last_near_recv_sem.at[group])
        for which in (LAST_DIRECT_A, LAST_DIRECT_B, LAST_SUM_A, LAST_SUM_B):
            arrived(last_in.at[group, which], last_recv_sem.at[group, which])
        top = last_near_in[group, pl.ds(0, 64)] + (last_in[group, LAST_SUM_A] + last_in[group, LAST_DIRECT_B])
        bottom = last_near_in[group, pl.ds(64, 64)] + (last_in[group, LAST_SUM_B] + last_in[group, LAST_DIRECT_A])
        rows = jnp.concatenate([top, bottom], 0).T
        for half in range(2):
            for part in range(2):
                swept[0, part, pl.ds(32 * group, 32), pl.ds(128 * half, 128)] = rows[32 * (2 * half + part) :][:32]

    def relay(step, group):
        last_relay(group) if step == STEPS - 1 else send_near(step, group)

    def take(step, group):
        last_take(group) if step == STEPS - 1 else take_near(step, group)

    for group in range(GROUPS):
        take_first(group)
        begin(0, group)
    send_far(0, 0)
    send_far(0, 1)
    for step in range(STEPS):
        for group in range(GROUPS):
            near_products(step, group)
        for group in range(GROUPS):
            relay(step, group)
        for group in range(GROUPS):
            take(step, group)
            if step + 1 < STEPS:
                begin(step + 1, group)
                send_far(step + 1, group)
    for copy in sent:
        copy.wait_send()

    @pl.when(jnp.logical_not(is_last))
    def _():
        for copy in sent_below:
            copy.wait_send()


def sweep(green_blocks, traces, sources):
    steps, dma = STEPS - 1, pltpu.SemaphoreType.DMA
    return pl.pallas_call(
        kernel,
        out_shape=jax.ShapeDtypeStruct(traces.shape, F32),
        in_specs=[pl.BlockSpec(memory_space=pltpu.HBM)] * 3,
        out_specs=pl.BlockSpec(memory_space=pltpu.VMEM),
        scratch_shapes=[
            pltpu.VMEM((2, CHIPS, 2, 256, 256), F32),
            pltpu.VMEM((CHIPS, 256, 2048), BF16),
            pltpu.VMEM((GROUPS, 2048, 256), BF16),
            pltpu.VMEM((2, 64, 256), F32),
            pltpu.VMEM((GROUPS, 2, 32, 256), F32),
            pltpu.VMEM((STEPS, GROUPS, 128, 128), F32),
            pltpu.VMEM((STEPS, GROUPS, 128, 128), F32),
            pltpu.VMEM((GROUPS, 2, 128, 128), F32),
            pltpu.VMEM((steps, GROUPS, 2, 128, 128), F32),
            pltpu.VMEM((steps, GROUPS, 2, 128, 128), F32),
            pltpu.VMEM((GROUPS, 2, 128, 128), F32),
            pltpu.VMEM((steps, GROUPS, 2, 128, 128), F32),
            pltpu.VMEM((steps, GROUPS, 2, 128, 128), F32),
            pltpu.VMEM((GROUPS, 128, 128), F32),
            pltpu.VMEM((GROUPS, 6, 64, 128), F32),
            pltpu.VMEM((GROUPS, 6, 64, 128), F32),
            pltpu.VMEM((GROUPS, 128, 128), F32),
            pltpu.VMEM((GROUPS, 128, 128), F32),
            dma((CHIPS,)), dma((CHIPS,)), dma((CHIPS,)), dma, dma, dma((GROUPS,)), dma((GROUPS,)),
            dma((STEPS, GROUPS)), dma((STEPS, GROUPS)),
            dma((steps, GROUPS, 2, PIECES)), dma((steps, GROUPS, 2, PIECES)),
            dma((steps, GROUPS, 2, PIECES)), dma((steps, GROUPS, 2, PIECES)),
            dma((GROUPS, 6)), dma((GROUPS, 6)), dma((GROUPS,)), dma((GROUPS,)),
        ],
        compiler_params=pltpu.CompilerParams(
            collective_id=0, has_side_effects=True, vmem_limit_bytes=67043328
        ),
        name="sweep",
    )(green_blocks, traces, sources)


def solution(mesh):
    placed = P("slab", None, None, "col")
    return jax.shard_map(sweep, mesh=mesh, in_specs=(placed,) * 3, out_specs=placed, check_vma=False)
```
